512 devices in a mesh: dp: 64 (over y, z), factor: 8 (over x, core).
Axes of the slice: x: 4, y: 8, z: 8, core: 2. Of those that a mesh axis runs over, the one named last changes fastest.
Arguments:
- layer_inputs: bfloat16 [65536, 5120], P('dp', 'factor'), may hold values from -64 to 64
- out_grads: bfloat16 [65536, 5120], P('dp', 'factor'), may hold values from -64 to 64
- weight_grad: bfloat16 [5120, 5120], P('dp', 'factor'), may hold values from -32 to 32
- left_inv: float32 [5120, 5120], P('dp', 'factor'), may hold values from -4 to 10, as said below
- right_inv: float32 [5120, 5120], P('factor', 'dp'), may hold values from -4 to 10, as said below
Outputs:
- precond_grad: bfloat16 [5120, 5120], P('dp', 'factor')
- new_left: float32 [5120, 5120], P('dp', 'factor')
- new_right: float32 [5120, 5120], P('factor', 'dp')
The draws below stay inside these ranges and needn't reach their ends.
Inputs may be any that keep to these rules, and one draw needn't show every extreme that they name: `left_inv`: symmetric and positive definite, every eigenvalue 0.1 or more. `right_inv`: symmetric and positive definite, every eigenvalue 0.1 or more.
All inputs are finite; a program needn't handle non-finite values.
Results may differ from the reference program's by a relative error of at most 0.00275.
The reference program's roundings to bfloat16 on the way (of `hidden`) count: a program that leaves them out, or rounds other values in their place, can miss the bound.
Values may be sent and summed in bfloat16 or wider, within the bound.
No kernel may reach another device: no remote copies, remote signals or barrier semaphores. Data moves between devices by JAX's collectives and lax.ppermute only.
A program may use at most 64 MiB of HBM per device.

```python
import math
import jax
import jax.numpy as jnp
from jax import lax

D = 5120
TOK_DEV = 1024
TOKENS = 65536


def column_ramp_values():
    return jnp.exp(jnp.arange(D, dtype=jnp.float32) / max(D - 1, 1) * math.log(10.0))


def mean_dirs(key):
    key_amag, key_asign, key_gmag, key_gsign = jax.random.split(jax.random.fold_in(key, 4021), 4)
    column_ramp = column_ramp_values()
    act_mag = jnp.exp(jax.random.uniform(key_amag, (D,), jnp.float32, math.log(0.1), math.log(1.0)))
    grad_mag = jnp.exp(jax.random.uniform(key_gmag, (D,), jnp.float32, math.log(0.1), math.log(1.0)))
    act_centre = jax.random.rademacher(key_asign, (D,), dtype=jnp.float32) * act_mag * column_ramp
    grad_centre = jax.random.rademacher(key_gsign, (D,), dtype=jnp.float32) * grad_mag * column_ramp
    return (act_centre, grad_centre)


def token_rows(key, centre):
    key_noise, key_omag, key_osign = jax.random.split(key, 3)
    block_count = TOKENS // TOK_DEV
    column_ramp = column_ramp_values()
    offset_mag = jnp.exp(jax.random.uniform(key_omag, (block_count, D), jnp.float32, math.log(0.1), math.log(1.0)))
    offsets = jax.random.rademacher(key_osign, (block_count, D), dtype=jnp.float32) * offset_mag * column_ramp[None, :]
    row_offsets = jnp.repeat(offsets, TOK_DEV, axis=0, total_repeat_length=TOKENS)
    position = jnp.arange(TOKENS, dtype=jnp.float32) / max(TOKENS - 1, 1)
    row_scale = jnp.exp(position * math.log(3.0))
    noise = jnp.clip(jax.random.normal(key_noise, (TOKENS, D), jnp.float32), -5.0, 5.0)
    return jnp.clip(row_scale[:, None] * (centre[None, :] + row_offsets + noise), -64.0, 64.0)


def draw_layer_inputs(key, part):
    act_centre, grad_centre = mean_dirs(key)
    return token_rows(jax.random.fold_in(key, 31), act_centre).astype(jnp.bfloat16)


def draw_out_grads(key, part):
    act_centre, grad_centre = mean_dirs(key)
    return token_rows(jax.random.fold_in(key, 37), grad_centre).astype(jnp.bfloat16)


def draw_weight_grad(key, part):
    act_centre, grad_centre = mean_dirs(key)
    key_left, key_right, key_noise = jax.random.split(jax.random.fold_in(key, 41), 3)
    left_dir = act_centre / jnp.sqrt(jnp.mean(act_centre * act_centre))
    right_dir = grad_centre / jnp.sqrt(jnp.mean(grad_centre * grad_centre))
    left_mix = jnp.clip(jax.random.normal(key_left, (D,), jnp.float32), -4.0, 4.0)
    right_mix = jnp.clip(jax.random.normal(key_right, (D,), jnp.float32), -4.0, 4.0)
    noise = 0.25 * jnp.clip(jax.random.normal(key_noise, (D, D), jnp.float32), -5.0, 5.0)
    full = noise + left_dir[:, None] * left_mix[None, :] + right_mix[:, None] * right_dir[None, :]
    return jnp.clip(full, -32.0, 32.0).astype(jnp.bfloat16)


def definite(key):
    key_base = jax.random.fold_in(key, 0)
    base = jax.random.normal(key_base, (D, D), jnp.float32)
    product = jnp.dot(base, base.T, precision=lax.Precision.HIGHEST) / D
    matrix = 0.5 * jnp.eye(D, dtype=jnp.float32) + 0.5 * (product + product.T)
    return jnp.clip(matrix, -4.0, 10.0)


def draw_left_inv(key, part):
    return definite(jax.random.fold_in(key, 13))


def draw_right_inv(key, part):
    return definite(jax.random.fold_in(key, 17))


def setup_inputs(seed: int = 0) -> dict:
    seeds = jax.random.split(jax.random.key(seed), 6)
    layer_inputs = draw_layer_inputs(jax.random.fold_in(seeds[5], 71), 0)
    out_grads = draw_out_grads(jax.random.fold_in(seeds[5], 71), 0)
    weight_grad = draw_weight_grad(jax.random.fold_in(seeds[5], 71), 0)
    left_inv = draw_left_inv(jax.random.fold_in(seeds[5], 71), 0)
    right_inv = draw_right_inv(jax.random.fold_in(seeds[5], 71), 0)
    return {"layer_inputs": layer_inputs, "out_grads": out_grads, "weight_grad": weight_grad, "left_inv": left_inv, "right_inv": right_inv}


decay = 0.9


def coefficient(quadratic):
    return (1.0 - decay) / (decay * decay * (1.0 + (1.0 - decay) / decay * quadratic))


def reference(layer_inputs, out_grads, weight_grad, left_inv, right_inv):
    token_count = layer_inputs.shape[0]
    mean_act = jnp.sum(layer_inputs, axis=0, dtype=jnp.float32) / token_count
    mean_grad = jnp.sum(out_grads, axis=0, dtype=jnp.float32) / token_count
    left_image = jnp.dot(left_inv, mean_act, precision=lax.Precision.HIGHEST)
    right_image = jnp.dot(right_inv, mean_grad, precision=lax.Precision.HIGHEST)
    left_quad = jnp.sum(mean_act * left_image)
    right_quad = jnp.sum(mean_grad * right_image)
    left_coef = coefficient(left_quad)
    right_coef = coefficient(right_quad)
    new_left = left_inv / decay - left_coef * left_image[:, None] * left_image[None, :]
    new_right = right_inv / decay - right_coef * right_image[:, None] * right_image[None, :]
    left_half = new_left.astype(jnp.bfloat16)
    right_half = new_right.astype(jnp.bfloat16)
    hidden = jnp.dot(left_half, weight_grad, preferred_element_type=jnp.float32).astype(jnp.bfloat16)
    precond_grad = jnp.dot(hidden, right_half, preferred_element_type=jnp.float32).astype(jnp.bfloat16)
    return precond_grad, new_left, new_right
```

```python
import jax
import jax.numpy as jnp
from jax import lax
from jax.sharding import Mesh, PartitionSpec as P

decay = 0.9
PAD = 104


def coefficient(quadratic):
    return (1.0 - decay) / (decay * decay * (1.0 + (1.0 - decay) / decay * quadratic))


def share(vec, axes, count):
    return lax.all_to_all(jnp.broadcast_to(vec[None], (count,) + vec.shape), axes, 0, 0, tiled=True)


def gather_rows(block, axis, count):
    rows, cols = block.shape
    padded = jnp.pad(block, ((0, PAD - rows), (0, 0)))
    whole = lax.all_gather(padded, axis, axis=0, tiled=False)
    return whole[:, :rows, :].reshape(count * rows, cols)


def per_device(layer_inputs, out_grads, weight_grad, left_inv, right_inv):
    ny, nz, nf = lax.axis_size("y"), lax.axis_size("z"), lax.axis_size("f")
    token_count = layer_inputs.shape[0] * ny * nz
    rows, cols = left_inv.shape
    y, z, f = lax.axis_index("y"), lax.axis_index("z"), lax.axis_index("f")

    left_wide = lax.all_gather(left_inv, "y", axis=0, tiled=True)
    swap = [(a * nf + b, b * nf + a) for a in range(ny) for b in range(nf)]
    weight_piece = lax.ppermute(weight_grad, ("y", "f"), swap)

    act_local = jnp.sum(layer_inputs, axis=0, dtype=jnp.float32)
    grad_local = jnp.sum(out_grads, axis=0, dtype=jnp.float32)
    sums = share(jnp.concatenate([act_local, grad_local]), ("y", "z"), ny * nz)
    means = jnp.sum(sums, axis=0) / token_count
    mean_act, mean_grad = means[:cols], means[cols:]

    weight_piece, means = lax.optimization_barrier((weight_piece, means))
    weight_block = gather_rows(weight_piece, "z", nz)

    left_partial = jnp.sum(left_inv * means[None, :cols], axis=1)
    right_partial = jnp.sum(right_inv * means[cols:, None], axis=0)
    both = share(jnp.concatenate([means, left_partial, right_partial]), "f", nf)
    whole_act = both[:, :cols].reshape(nf * cols)
    whole_grad = both[:, cols : 2 * cols].reshape(nf * cols)
    images = jnp.sum(both[:, 2 * cols :], axis=0)

    all_images = share(images, ("y", "z"), ny * nz)
    left_image = all_images[:, :rows].reshape(ny * nz * rows)
    right_image = all_images[:, rows:].reshape(ny * nz * rows)
    left_coef = coefficient(jnp.sum(whole_act * left_image))
    right_coef = coefficient(jnp.sum(whole_grad * right_image))

    left_cols = lax.dynamic_slice_in_dim(left_image, f * cols, cols)
    right_rows = lax.dynamic_slice_in_dim(right_image, f * cols, cols)
    new_left = left_inv / decay - left_coef * images[:rows, None] * left_cols[None, :]
    new_right = right_inv / decay - right_coef * right_rows[:, None] * images[None, rows:]

    right_block = gather_rows(new_right.astype(jnp.bfloat16).T, "z", nz)

    wide_rows = lax.dynamic_slice_in_dim(left_image.reshape(ny, nz, rows), z, 1, 1).reshape(ny * rows)
    left_block = left_wide / decay - left_coef * wide_rows[:, None] * left_cols[None, :]
    partial = jnp.dot(
        left_block.astype(jnp.bfloat16), weight_block, preferred_element_type=jnp.float32
    )
    pieces = lax.all_to_all(partial.reshape(nf, ny * rows // nf, cols), "f", 0, 0, tiled=True)
    hidden_piece = jnp.sum(pieces, axis=0).astype(jnp.bfloat16)
    hidden = lax.all_gather(hidden_piece, "f", axis=0, tiled=True)

    partial = jnp.dot(hidden, right_block, preferred_element_type=jnp.float32)
    pieces = lax.all_to_all(partial.reshape(ny, rows, cols), "y", 0, 0, tiled=True)
    precond = jnp.sum(pieces, axis=0).astype(jnp.bfloat16)
    return (precond, new_left, new_right)


def solution(mesh):
    cube = Mesh(mesh.devices.reshape(8, 8, 8), ("y", "z", "f"))
    rows, cols = P(("y", "z"), "f"), P("f", ("y", "z"))
    return jax.shard_map(
        per_device,
        mesh=cube,
        in_specs=(rows, rows, rows, rows, cols),
        out_specs=(rows, rows, cols),
        check_vma=False,
    )
```

```python
import jax
import jax.numpy as jnp
from jax import lax
from jax.sharding import Mesh, PartitionSpec as P


decay = 0.9
Y = ("u", "v")
F = ("x", "c")
DP = ("u", "v", "z")


def coefficient(quadratic):
    return (1.0 - decay) / (decay * decay * (1.0 + (1.0 - decay) / decay * quadratic))


def share(vec, axes):
    count = lax.axis_size(axes)
    return lax.all_to_all(jnp.broadcast_to(vec[None], (count,) + vec.shape), axes, 0, 0, tiled=True)


def per_device(layer_inputs, out_grads, weight_grad, left_inv, right_inv):
    ny, nz, nf, nx = lax.axis_size(Y), lax.axis_size("z"), lax.axis_size(F), lax.axis_size("x")
    nu = lax.axis_size("u")
    token_count = layer_inputs.shape[0] * ny * nz
    rows, cols = left_inv.shape
    half = rows // 2
    u, v, z, f = lax.axis_index("u"), lax.axis_index("v"), lax.axis_index("z"), lax.axis_index(F)

    left_wide = lax.all_gather(left_inv, Y, axis=0, tiled=False)
    swap = [(a * nf + b, b * nf + a) for a in range(ny) for b in range(nf)]
    weight_piece = lax.ppermute(weight_grad, Y + F, swap)
    right_rows_own = right_inv.T
    right_other = lax.ppermute(right_rows_own, "v", [(0, 1), (1, 0)])
    right_pair = jnp.concatenate([right_rows_own[None], right_other[None]], axis=0)

    act_local = jnp.sum(layer_inputs, axis=0, dtype=jnp.float32)
    grad_local = jnp.sum(out_grads, axis=0, dtype=jnp.float32)
    sums = share(jnp.concatenate([act_local, grad_local]), DP)
    means = jnp.sum(sums, axis=0) / token_count

    weight_piece, right_pair, means = lax.optimization_barrier((weight_piece, right_pair, means))
    weight_block = share(weight_piece, "z").reshape(nz * rows, cols)
    right_wide = lax.all_gather(right_pair, "z", axis=0, tiled=False)

    left_partial = jnp.sum(left_inv * means[None, :cols], axis=1)
    right_partial = jnp.sum(right_inv * means[cols:, None], axis=0)
    both = share(jnp.concatenate([means, left_partial, right_partial]), F)
    whole_act = both[:, :cols].reshape(nf * cols)
    whole_grad = both[:, cols : 2 * cols].reshape(nf * cols)
    images = jnp.sum(both[:, 2 * cols :], axis=0)
    all_images = share(images, DP)
    left_image = all_images[:, :rows].reshape(ny * nz * rows)
    right_image = all_images[:, rows:].reshape(ny * nz * rows)
    left_coef = coefficient(jnp.sum(whole_act * left_image))
    right_coef = coefficient(jnp.sum(whole_grad * right_image))

    left_cols = lax.dynamic_slice_in_dim(left_image, f * cols, cols)
    right_cols = lax.dynamic_slice_in_dim(right_image, f * cols, cols)

    wide_image = lax.dynamic_slice_in_dim(left_image.reshape(ny, nz, rows), z, 1, 1)
    left_block = left_wide / decay - (left_coef * wide_image.reshape(ny, rows, 1)) * left_cols
    left_half = left_block.astype(jnp.bfloat16).reshape(nx, 2, 2, half, cols)
    left_half = left_half.transpose(0, 2, 1, 3, 4).reshape(ny * rows, cols)
    partial = jnp.dot(left_half, weight_block, preferred_element_type=jnp.float32)
    pieces = lax.all_to_all(partial.reshape(nf, 2, half, cols), F, 0, 0, tiled=True)
    hidden_piece = jnp.sum(pieces, axis=0).astype(jnp.bfloat16)
    hidden_piece = lax.all_to_all(hidden_piece, "v", 0, 0, tiled=True)
    hidden_piece = hidden_piece.transpose(1, 0, 2).reshape(half, 2 * cols)
    hidden = lax.all_gather(hidden_piece, F, axis=0, tiled=True)

    pair_image = lax.dynamic_slice_in_dim(right_image.reshape(nu, 2, nz, rows), u, 1, 0)[0]
    right_sorted = jnp.where(v == 0, right_wide, right_wide[:, ::-1]).transpose(1, 0, 2, 3)
    right_block = right_sorted / decay - (right_coef * pair_image[..., None]) * right_cols
    right_half = right_block.astype(jnp.bfloat16).reshape(2 * nz * rows, cols)
    partial = jnp.dot(hidden, right_half, preferred_element_type=jnp.float32)
    pieces = lax.all_to_all(partial.reshape(nu, rows, cols), "u", 0, 0, tiled=True)
    precond = jnp.sum(pieces, axis=0).astype(jnp.bfloat16)

    new_left = left_inv / decay - left_coef * images[:rows, None] * left_cols[None, :]
    new_right = right_inv / decay - right_coef * right_cols[:, None] * images[None, rows:]
    return (precond, new_left, new_right)


def solution(mesh):
    cube = Mesh(mesh.devices.reshape(4, 2, 8, 4, 2), ("u", "v", "z", "x", "c"))
    rows, cols = P(DP, F), P(F, DP)

    return jax.shard_map(
        per_device,
        mesh=cube,
        in_specs=(rows, rows, rows, rows, cols),
        out_specs=(rows, rows, cols),
        check_vma=False,
    )
```

```python
import jax
import jax.numpy as jnp
from jax import lax
from jax.sharding import Mesh, PartitionSpec as P


decay = 0.9
PAD = 104
Y = ("u", "v")
F = ("x", "c")
DP = ("u", "v", "z")


def coefficient(quadratic):
    return (1.0 - decay) / (decay * decay * (1.0 + (1.0 - decay) / decay * quadratic))


def share(vec, axes):
    count = lax.axis_size(axes)
    return lax.all_to_all(jnp.broadcast_to(vec[None], (count,) + vec.shape), axes, 0, 0, tiled=True)


def per_device(layer_inputs, out_grads, weight_grad, left_inv, right_inv):
    ny, nz, nf, nx = lax.axis_size(Y), lax.axis_size("z"), lax.axis_size(F), lax.axis_size("x")
    nu = lax.axis_size("u")
    token_count = layer_inputs.shape[0] * ny * nz
    rows, cols = left_inv.shape
    half = rows // 2
    v, z, f = lax.axis_index("v"), lax.axis_index("z"), lax.axis_index(F)

    left_wide = lax.all_gather(left_inv, Y, axis=0, tiled=False)
    swap = [(a * nf + b, b * nf + a) for a in range(ny) for b in range(nf)]
    weight_piece = lax.ppermute(weight_grad, Y + F, swap)
    act_local = jnp.sum(layer_inputs, axis=0, dtype=jnp.float32)
    grad_local = jnp.sum(out_grads, axis=0, dtype=jnp.float32)
    sums = share(jnp.concatenate([act_local, grad_local]), DP)
    means = jnp.sum(sums, axis=0) / token_count

    padded = jnp.pad(weight_piece, ((0, PAD - rows), (0, 0)))
    weight_wide = lax.all_gather(padded, "z", axis=0, tiled=False)
    weight_block = weight_wide[:, :rows, :].reshape(nz * rows, cols)

    left_partial = jnp.sum(left_inv * means[None, :cols], axis=1)
    right_partial = jnp.sum(right_inv * means[cols:, None], axis=0)
    both = share(jnp.concatenate([means, left_partial, right_partial]), F)
    whole_act = both[:, :cols].reshape(nf * cols)
    whole_grad = both[:, cols : 2 * cols].reshape(nf * cols)
    images = jnp.sum(both[:, 2 * cols :], axis=0)
    all_images = share(images, DP)
    left_image = all_images[:, :rows].reshape(ny * nz * rows)
    right_image = all_images[:, rows:].reshape(ny * nz * rows)
    left_coef = coefficient(jnp.sum(whole_act * left_image))
    right_coef = coefficient(jnp.sum(whole_grad * right_image))

    left_cols = lax.dynamic_slice_in_dim(left_image, f * cols, cols)
    right_cols = lax.dynamic_slice_in_dim(right_image, f * cols, cols)

    new_left = left_inv / decay - left_coef * images[:rows, None] * left_cols[None, :]
    new_right = right_inv / decay - right_coef * right_cols[:, None] * images[None, rows:]

    right_own = new_right.astype(jnp.bfloat16).T
    right_other = lax.ppermute(right_own, "v", [(0, 1), (1, 0)])
    right_pair = jnp.where(
        v == 0, jnp.stack([right_own, right_other]), jnp.stack([right_other, right_own])
    )
    right_wide = lax.all_gather(right_pair, "z", axis=0, tiled=False)
    right_half = right_wide.transpose(1, 0, 2, 3).reshape(2 * nz * rows, cols)

    wide_image = lax.dynamic_slice_in_dim(left_image.reshape(ny, nz, rows), z, 1, 1)
    left_block = left_wide / decay - (left_coef * wide_image.reshape(ny, rows, 1)) * left_cols
    left_half = left_block.astype(jnp.bfloat16).reshape(nx, 2, 2, half, cols)
    left_half = left_half.transpose(0, 2, 1, 3, 4).reshape(ny * rows, cols)
    partial = jnp.dot(left_half, weight_block, preferred_element_type=jnp.float32)
    pieces = lax.all_to_all(partial.reshape(nf, 2, half, cols), F, 0, 0, tiled=True)
    hidden_piece = jnp.sum(pieces, axis=0).astype(jnp.bfloat16)
    hidden_piece = lax.all_to_all(hidden_piece, "v", 0, 0, tiled=True)
    hidden_piece = hidden_piece.transpose(1, 0, 2).reshape(half, 2 * cols)
    hidden = lax.all_gather(hidden_piece, F, axis=0, tiled=True)

    partial = jnp.dot(hidden, right_half, preferred_element_type=jnp.float32)
    pieces = lax.all_to_all(partial.reshape(nu, rows, cols), "u", 0, 0, tiled=True)
    precond = jnp.sum(pieces, axis=0).astype(jnp.bfloat16)

    return (precond, new_left, new_right)


def solution(mesh):
    cube = Mesh(mesh.devices.reshape(4, 2, 8, 4, 2), ("u", "v", "z", "x", "c"))
    rows, cols = P(DP, F), P(F, DP)

    return jax.shard_map(
        per_device,
        mesh=cube,
        in_specs=(rows, rows, rows, rows, cols),
        out_specs=(rows, rows, cols),
        check_vma=False,
    )
```

```python
import jax
import jax.numpy as jnp
from jax import lax
from jax.sharding import Mesh, PartitionSpec as P


decay = 0.9
PAD = 104
F = ("x", "c")
DP = ("u", "v", "z")


def coefficient(quadratic):
    return (1.0 - decay) / (decay * decay * (1.0 + (1.0 - decay) / decay * quadratic))


def share(vec, axes):
    count = lax.axis_size(axes)
    return lax.all_to_all(jnp.broadcast_to(vec[None], (count,) + vec.shape), axes, 0, 0, tiled=True)


def swap_u_x(block):
    n = lax.axis_size("u")
    return lax.ppermute(block, ("u", "x"), [(a * n + b, b * n + a) for a in range(n) for b in range(n)])


def swap_v(block):
    return lax.ppermute(block, "v", [(0, 1), (1, 0)])


def block_of(vec, index, size):
    return lax.dynamic_slice_in_dim(vec, index * size, size)


def per_device(layer_inputs, out_grads, weight_grad, left_inv, right_inv):
    nu, nz, nf, ndp = lax.axis_size("u"), lax.axis_size("z"), lax.axis_size(F), lax.axis_size(DP)
    token_count = layer_inputs.shape[0] * ndp
    rows, cols = left_inv.shape
    u, v, z, f = lax.axis_index("u"), lax.axis_index("v"), lax.axis_index("z"), lax.axis_index(F)

    padded = jnp.pad(weight_grad, ((0, PAD - rows), (0, 0)))
    weight_wide = lax.all_gather(padded, "z", axis=0, tiled=False)

    left_piece = swap_u_x(left_inv)
    left_wide = lax.all_gather(left_piece, F, axis=0, tiled=False)

    act_local = jnp.sum(layer_inputs, axis=0, dtype=jnp.float32)
    grad_local = jnp.sum(out_grads, axis=0, dtype=jnp.float32)
    sums = share(jnp.concatenate([act_local, grad_local]), DP)
    means = jnp.sum(sums, axis=0) / token_count

    left_partial = jnp.sum(left_inv * means[None, :cols], axis=1)
    right_partial = jnp.sum(right_inv * means[cols:, None], axis=0)
    both = share(jnp.concatenate([means, left_partial, right_partial]), F)
    whole_act = both[:, :cols].reshape(nf * cols)
    whole_grad = both[:, cols : 2 * cols].reshape(nf * cols)
    images = jnp.sum(both[:, 2 * cols :], axis=0)
    weight_wide, images = lax.optimization_barrier((weight_wide, images))
    weight_own = weight_wide[:, :rows, :].reshape(nz * rows, cols)
    weight_other = swap_v(weight_own)
    all_images = share(images, DP)
    left_image = all_images[:, :rows].reshape(ndp * rows)
    right_image = all_images[:, rows:].reshape(ndp * rows)
    left_coef = coefficient(jnp.sum(whole_act * left_image))
    right_coef = coefficient(jnp.sum(whole_grad * right_image))

    left_cols = block_of(left_image, f, cols)
    right_cols = block_of(right_image, f, cols)
    new_left = left_inv / decay - left_coef * images[:rows, None] * left_cols[None, :]
    new_right = right_inv / decay - right_coef * right_cols[:, None] * images[None, rows:]

    right_own = new_right.astype(jnp.bfloat16).T
    right_other = swap_v(right_own)
    right_pair = jnp.where(
        v == 0, jnp.stack([right_own, right_other]), jnp.stack([right_other, right_own])
    )
    right_wide = lax.all_gather(right_pair, "z", axis=0, tiled=False)

    row_image = lax.dynamic_index_in_dim(
        left_image.reshape(nu, ndp // nu, rows), v * nz + z, 1, keepdims=False
    )
    left_wide = left_wide.reshape(nu, 2, rows, cols)

    def left_half(which):
        old = lax.dynamic_index_in_dim(left_wide, which, 1, keepdims=False)
        col_image = block_of(left_image, 2 * u + which, cols)
        new = old / decay - (left_coef * row_image[:, :, None]) * col_image[None, None, :]
        return new.astype(jnp.bfloat16).reshape(nu * rows, cols)

    partial = jnp.dot(left_half(v), weight_own, preferred_element_type=jnp.float32)
    partial += jnp.dot(left_half(1 - v), weight_other, preferred_element_type=jnp.float32)
    pieces = lax.all_to_all(partial.reshape(nu, rows, cols), "u", 0, 0, tiled=True)
    hidden_piece = jnp.sum(pieces, axis=0).astype(jnp.bfloat16)
    hidden = lax.all_gather(hidden_piece, "u", axis=0, tiled=True)

    right_half = right_wide.transpose(1, 0, 2, 3).reshape(2, nz * rows, cols)
    partial = jnp.einsum(
        "crk,cmk->crm",
        jnp.broadcast_to(hidden[None], (2,) + hidden.shape),
        right_half,
        preferred_element_type=jnp.float32,
    )
    pieces = lax.all_to_all(partial.reshape(nf, rows, cols), ("c", "x"), 0, 0, tiled=True)
    precond = jnp.sum(pieces, axis=0).astype(jnp.bfloat16)
    precond = swap_u_x(precond)
    return (precond, new_left, new_right)


def solution(mesh):
    cube = Mesh(mesh.devices.reshape(4, 2, 8, 4, 2), ("u", "v", "z", "x", "c"))
    rows, cols = P(DP, F), P(F, DP)

    return jax.shard_map(
        per_device,
        mesh=cube,
        in_specs=(rows, rows, rows, rows, cols),
        out_specs=(rows, rows, cols),
        check_vma=False,
    )
```

```python
import jax
import jax.numpy as jnp
from jax import lax
from jax.sharding import Mesh, PartitionSpec as P


decay = 0.9
F = ("x", "c")
DP = ("u", "v", "z")


def coefficient(quadratic):
    return (1.0 - decay) / (decay * decay * (1.0 + (1.0 - decay) / decay * quadratic))


def share(vec, axes):
    count = lax.axis_size(axes)
    return lax.all_to_all(jnp.broadcast_to(vec[None], (count,) + vec.shape), axes, 0, 0, tiled=True)


def swap_u_x(block, flip):
    n, m = lax.axis_size("u"), lax.axis_size("v")
    moves = [
        ((a * m + w) * n + b, (b * m + (w + flip) % m) * n + a)
        for a in range(n)
        for w in range(m)
        for b in range(n)
    ]
    return lax.ppermute(block, ("u", "v", "x"), moves)


def in_order(own, other):
    return jnp.where(lax.axis_index("v") == 0, jnp.stack([own, other]), jnp.stack([other, own]))


def block_of(vec, index, size):
    return lax.dynamic_slice_in_dim(vec, index * size, size)


def per_device(layer_inputs, out_grads, weight_grad, left_inv, right_inv):
    nu, nv, nz = lax.axis_size("u"), lax.axis_size("v"), lax.axis_size("z")
    nf, ndp = lax.axis_size(F), lax.axis_size(DP)
    token_count = layer_inputs.shape[0] * ndp
    rows, cols = left_inv.shape
    _, z, x, f = (lax.axis_index(axes) for axes in ("u", "z", "x", F))

    weight_pieces = [swap_u_x(weight_grad, flip) for flip in range(2)]
    right_pieces = [swap_u_x(right_inv.T, flip) for flip in range(2)]

    act_local = jnp.sum(layer_inputs, axis=0, dtype=jnp.float32)
    grad_local = jnp.sum(out_grads, axis=0, dtype=jnp.float32)
    sums = share(jnp.concatenate([act_local, grad_local]), DP)
    means = jnp.sum(sums, axis=0) / token_count

    weight_pieces, _ = lax.optimization_barrier((weight_pieces, means))
    weight_wide = lax.all_gather(in_order(*weight_pieces), "z", axis=0, tiled=False)
    weight_wide = weight_wide.transpose(1, 0, 2, 3).reshape(nv * nz * rows, cols)

    left_partial = jnp.sum(left_inv * means[None, :cols], axis=1)
    right_partial = jnp.sum(right_inv * means[cols:, None], axis=0)
    both = share(jnp.concatenate([means, left_partial, right_partial]), F)
    whole_act = both[:, :cols].reshape(nf * cols)
    whole_grad = both[:, cols : 2 * cols].reshape(nf * cols)
    images = jnp.sum(both[:, 2 * cols :], axis=0)
    all_images = share(images, DP)
    left_image = all_images[:, :rows].reshape(ndp * rows)
    right_image = all_images[:, rows:].reshape(ndp * rows)
    left_coef = coefficient(jnp.sum(whole_act * left_image))
    right_coef = coefficient(jnp.sum(whole_grad * right_image))

    left_cols = block_of(left_image, f, cols)
    right_cols = block_of(right_image, f, cols)
    new_left = left_inv / decay - left_coef * images[:rows, None] * left_cols[None, :]
    new_right = right_inv / decay - right_coef * right_cols[:, None] * images[None, rows:]

    row_image = right_image.reshape(nu, nv, nz, rows)[x, :, z]
    col_image = block_of(right_image, lax.axis_index(("u", "c")), cols)
    right_pair = in_order(*right_pieces) / decay - (right_coef * col_image) * row_image[:, :, None]
    right_wide = lax.all_gather(right_pair.astype(jnp.bfloat16), "z", axis=0, tiled=False)

    left_wide = lax.all_gather(new_left.astype(jnp.bfloat16), ("c", "u"), axis=0, tiled=True)
    left_wide = left_wide.reshape(2, nu * rows, cols).transpose(1, 0, 2).reshape(nu * rows, 2 * cols)
    partial = jnp.dot(left_wide, weight_wide, preferred_element_type=jnp.float32)
    pieces = lax.all_to_all(partial.reshape(nu, rows, cols), "x", 0, 0, tiled=True)
    hidden_piece = jnp.sum(pieces, axis=0).astype(jnp.bfloat16)
    hidden = lax.all_gather(hidden_piece, "x", axis=0, tiled=True)

    right_half = right_wide.transpose(1, 0, 2, 3).reshape(nv, nz * rows, cols)
    partial = jnp.einsum(
        "crk,cmk->crm",
        jnp.broadcast_to(hidden[None], (nv,) + hidden.shape),
        right_half,
        preferred_element_type=jnp.float32,
    )
    pieces = lax.all_to_all(partial, "c", 0, 0, tiled=True)
    partial = jnp.sum(pieces, axis=0)
    pieces = lax.all_to_all(partial.reshape(nu, rows, cols), "u", 0, 0, tiled=True)
    precond = jnp.sum(pieces, axis=0).astype(jnp.bfloat16)
    return (precond, new_left, new_right)


def solution(mesh):
    cube = Mesh(mesh.devices.reshape(4, 2, 8, 4, 2), ("u", "v", "z", "x", "c"))
    rows, cols = P(DP, F), P(F, DP)

    return jax.shard_map(
        per_device,
        mesh=cube,
        in_specs=(rows, rows, rows, rows, cols),
        out_specs=(rows, rows, cols),
        check_vma=False,
    )
```

```python
import jax
import jax.numpy as jnp
from jax import lax
from jax.sharding import Mesh, PartitionSpec as P


decay = 0.9
F = ("x", "c")
DP = ("u", "v", "z")


def coefficient(quadratic):
    return (1.0 - decay) / (decay * decay * (1.0 + (1.0 - decay) / decay * quadratic))


def share(vec, axes):
    count = lax.axis_size(axes)
    return lax.all_to_all(jnp.broadcast_to(vec[None], (count,) + vec.shape), axes, 0, 0, tiled=True)


def swap_u_x(block, flip):
    n, m = lax.axis_size("u"), lax.axis_size("v")
    moves = [
        ((a * m + w) * n + b, (b * m + (w + flip) % m) * n + a)
        for a in range(n)
        for w in range(m)
        for b in range(n)
    ]
    return lax.ppermute(block, ("u", "v", "x"), moves)


def in_order(own, other):
    return jnp.where(lax.axis_index("v") == 0, jnp.stack([own, other]), jnp.stack([other, own]))


def block_of(vec, index, size):
    return lax.dynamic_slice_in_dim(vec, index * size, size)


def per_device(layer_inputs, out_grads, weight_grad, left_inv, right_inv):
    nu, nv, nz = lax.axis_size("u"), lax.axis_size("v"), lax.axis_size("z")
    nf, ndp = lax.axis_size(F), lax.axis_size(DP)
    token_count = layer_inputs.shape[0] * ndp
    rows, cols = left_inv.shape
    v, z, x, f = (lax.axis_index(axes) for axes in ("v", "z", "x", F))

    left_wide = lax.all_gather(left_inv, ("c", "u"), axis=0, tiled=False)

    weight_pieces = [swap_u_x(weight_grad, flip) for flip in range(2)]
    right_pieces = [swap_u_x(right_inv.T, flip) for flip in range(2)]

    act_local = jnp.sum(layer_inputs, axis=0, dtype=jnp.float32)
    grad_local = jnp.sum(out_grads, axis=0, dtype=jnp.float32)
    sums = share(jnp.concatenate([act_local, grad_local]), DP)
    means = jnp.sum(sums, axis=0) / token_count

    weight_pieces, _ = lax.optimization_barrier((weight_pieces, means))
    weight_wide = lax.all_gather(in_order(*weight_pieces), "z", axis=0, tiled=False)
    weight_wide = weight_wide.transpose(1, 0, 2, 3).reshape(nv * nz * rows, cols)

    left_partial = jnp.sum(left_inv * means[None, :cols], axis=1)
    right_partial = jnp.sum(right_inv * means[cols:, None], axis=0)
    both = share(jnp.concatenate([means, left_partial, right_partial]), F)
    whole_act = both[:, :cols].reshape(nf * cols)
    whole_grad = both[:, cols : 2 * cols].reshape(nf * cols)
    images = jnp.sum(both[:, 2 * cols :], axis=0)
    all_images = share(images, DP)
    left_image = all_images[:, :rows].reshape(ndp * rows)
    right_image = all_images[:, rows:].reshape(ndp * rows)
    left_coef = coefficient(jnp.sum(whole_act * left_image))
    right_coef = coefficient(jnp.sum(whole_grad * right_image))

    left_cols = block_of(left_image, f, cols)
    right_cols = block_of(right_image, f, cols)
    new_left = left_inv / decay - left_coef * images[:rows, None] * left_cols[None, :]
    new_right = right_inv / decay - right_coef * right_cols[:, None] * images[None, rows:]

    row_image = right_image.reshape(nu, nv, nz, rows)[x, :, z]
    col_image = block_of(right_image, lax.axis_index(("u", "c")), cols)
    right_pair = in_order(*right_pieces) / decay - (right_coef * col_image) * row_image[:, :, None]
    right_wide = lax.all_gather(right_pair.astype(jnp.bfloat16), "z", axis=0, tiled=False)

    row_image = lax.dynamic_index_in_dim(
        left_image.reshape(nu, nv * nz, rows), v * nz + z, 1, keepdims=False
    )
    col_image = left_image.reshape(nu, 2, cols)[x]
    left_wide = left_wide.reshape(2, nu, rows, cols)
    left_wide = left_wide / decay - (left_coef * row_image[:, :, None]) * col_image[:, None, None, :]
    left_half = left_wide.astype(jnp.bfloat16).transpose(1, 2, 0, 3).reshape(nu * rows, 2 * cols)
    partial = jnp.dot(left_half, weight_wide, preferred_element_type=jnp.float32)
    pieces = lax.all_to_all(partial.reshape(nu, rows, cols), "x", 0, 0, tiled=True)
    hidden_piece = jnp.sum(pieces, axis=0).astype(jnp.bfloat16)
    hidden = lax.all_gather(hidden_piece, "x", axis=0, tiled=True)

    right_half = right_wide.transpose(1, 0, 2, 3).reshape(nv, nz * rows, cols)
    partial = jnp.einsum(
        "crk,cmk->crm",
        jnp.broadcast_to(hidden[None], (nv,) + hidden.shape),
        right_half,
        preferred_element_type=jnp.float32,
    )
    pieces = lax.all_to_all(partial, "c", 0, 0, tiled=True)
    partial = jnp.sum(pieces, axis=0)
    pieces = lax.all_to_all(partial.reshape(nu, rows, cols), "u", 0, 0, tiled=True)
    precond = jnp.sum(pieces, axis=0).astype(jnp.bfloat16)
    return (precond, new_left, new_right)


def solution(mesh):
    cube = Mesh(mesh.devices.reshape(4, 2, 8, 4, 2), ("u", "v", "z", "x", "c"))
    rows, cols = P(DP, F), P(F, DP)

    return jax.shard_map(
        per_device,
        mesh=cube,
        in_specs=(rows, rows, rows, rows, cols),
        out_specs=(rows, rows, cols),
        check_vma=False,
    )
```

```python
import jax
import jax.numpy as jnp
from jax import lax
from jax.sharding import Mesh, PartitionSpec as P


decay = 0.9
F = ("x", "c")
DP = ("u", "v", "z")


def coefficient(quadratic):
    return (1.0 - decay) / (decay * decay * (1.0 + (1.0 - decay) / decay * quadratic))


def share(vec, axes):
    count = lax.axis_size(axes)
    return lax.all_to_all(jnp.broadcast_to(vec[None], (count,) + vec.shape), axes, 0, 0, tiled=True)


def swap_u_x(block, flip):
    n, m = lax.axis_size("u"), lax.axis_size("v")
    moves = [
        ((a * m + w) * n + b, (b * m + (w + flip) % m) * n + a)
        for a in range(n)
        for w in range(m)
        for b in range(n)
    ]
    return lax.ppermute(block, ("u", "v", "x"), moves)


def swap_v_c(block, flip):
    moves = [(2 * a + b, 2 * ((b + flip) % 2) + a) for a in range(2) for b in range(2)]
    return lax.ppermute(block, ("v", "c"), moves)


def in_order(own, other):
    return jnp.where(lax.axis_index("v") == 0, jnp.stack([own, other]), jnp.stack([other, own]))


def block_of(vec, index, size):
    return lax.dynamic_slice_in_dim(vec, index * size, size)


def per_device(layer_inputs, out_grads, weight_grad, left_inv, right_inv):
    nu, nv, nz = lax.axis_size("u"), lax.axis_size("v"), lax.axis_size("z")
    nf, ndp = lax.axis_size(F), lax.axis_size(DP)
    token_count = layer_inputs.shape[0] * ndp
    rows, cols = left_inv.shape
    v, z, x, f = (lax.axis_index(axes) for axes in ("v", "z", "x", F))

    left_wide = lax.all_gather(left_inv, ("c", "u"), axis=0, tiled=False)

    weight_pieces = [swap_u_x(weight_grad, flip) for flip in range(2)]
    act_local = jnp.sum(layer_inputs, axis=0, dtype=jnp.float32)
    grad_local = jnp.sum(out_grads, axis=0, dtype=jnp.float32)
    sums = share(jnp.concatenate([act_local, grad_local]), DP)
    means = jnp.sum(sums, axis=0) / token_count

    left_partial = jnp.sum(left_inv * means[None, :cols], axis=1)
    right_partial = jnp.sum(right_inv * means[cols:, None], axis=0)
    both = share(jnp.concatenate([means, left_partial, right_partial]), F)
    whole_act = both[:, :cols].reshape(nf * cols)
    whole_grad = both[:, cols : 2 * cols].reshape(nf * cols)
    images = jnp.sum(both[:, 2 * cols :], axis=0)
    weight_pieces, _ = lax.optimization_barrier((weight_pieces, images))
    weight_wide = lax.all_gather(in_order(*weight_pieces), "z", axis=0, tiled=False)
    weight_wide = weight_wide.transpose(1, 0, 2, 3).reshape(nv * nz * rows, cols)
    all_images = share(images, DP)
    left_image = all_images[:, :rows].reshape(ndp * rows)
    right_image = all_images[:, rows:].reshape(ndp * rows)
    left_coef = coefficient(jnp.sum(whole_act * left_image))
    right_coef = coefficient(jnp.sum(whole_grad * right_image))

    left_cols = block_of(left_image, f, cols)
    right_cols = block_of(right_image, f, cols)
    new_left = left_inv / decay - left_coef * images[:rows, None] * left_cols[None, :]
    new_right = right_inv / decay - right_coef * right_cols[:, None] * images[None, rows:]

    right_own = new_right.astype(jnp.bfloat16).T
    right_pieces = [swap_v_c(right_own, flip) for flip in range(2)]
    right_wide = lax.all_gather(in_order(*right_pieces), "z", axis=0, tiled=False)

    row_image = lax.dynamic_index_in_dim(
        left_image.reshape(nu, nv * nz, rows), v * nz + z, 1, keepdims=False
    )
    col_image = left_image.reshape(nu, 2, cols)[x]
    left_wide = left_wide.reshape(2, nu, rows, cols)
    left_wide = left_wide / decay - (left_coef * row_image[:, :, None]) * col_image[:, None, None, :]
    left_half = left_wide.astype(jnp.bfloat16).transpose(1, 2, 0, 3).reshape(nu * rows, 2 * cols)
    partial = jnp.dot(left_half, weight_wide, preferred_element_type=jnp.float32)
    pieces = lax.all_to_all(partial.reshape(nu, rows, cols), "x", 0, 0, tiled=True)
    hidden_piece = jnp.sum(pieces, axis=0).astype(jnp.bfloat16)
    hidden = lax.all_gather(hidden_piece, "x", axis=0, tiled=True)

    right_half = right_wide.transpose(1, 0, 2, 3).reshape(nv, nz * rows, cols)
    partial = jnp.einsum(
        "crk,ckm->crm",
        jnp.broadcast_to(hidden[None], (nv,) + hidden.shape),
        right_half,
        preferred_element_type=jnp.float32,
    )
    pieces = lax.all_to_all(partial, "c", 0, 0, tiled=True)
    partial = jnp.sum(pieces, axis=0)
    pieces = lax.all_to_all(partial.reshape(nu, rows, cols), "u", 0, 0, tiled=True)
    precond = jnp.sum(pieces, axis=0).astype(jnp.bfloat16)
    return (precond, new_left, new_right)


def solution(mesh):
    cube = Mesh(mesh.devices.reshape(4, 2, 8, 4, 2), ("u", "v", "z", "x", "c"))
    rows, cols = P(DP, F), P(F, DP)

    return jax.shard_map(
        per_device,
        mesh=cube,
        in_specs=(rows, rows, rows, rows, cols),
        out_specs=(rows, rows, cols),
        check_vma=False,
    )
```

```python
import jax
import jax.numpy as jnp
from jax import lax
from jax.sharding import Mesh, PartitionSpec as P


decay = 0.9
PAD = 104
F = ("x", "c")
DP = ("u", "v", "z")


def coefficient(quadratic):
    return (1.0 - decay) / (decay * decay * (1.0 + (1.0 - decay) / decay * quadratic))


def share(vec, axes):
    count = lax.axis_size(axes)
    return lax.all_to_all(jnp.broadcast_to(vec[None], (count,) + vec.shape), axes, 0, 0, tiled=True)


def swap_u_x(block):
    n = lax.axis_size("u")
    return lax.ppermute(block, ("u", "x"), [(a * n + b, b * n + a) for a in range(n) for b in range(n)])


def swap_v(block):
    return lax.ppermute(block, "v", [(0, 1), (1, 0)])


def block_of(vec, index, size):
    return lax.dynamic_slice_in_dim(vec, index * size, size)


def per_device(layer_inputs, out_grads, weight_grad, left_inv, right_inv):
    nu, nz, nf, ndp = lax.axis_size("u"), lax.axis_size("z"), lax.axis_size(F), lax.axis_size(DP)
    token_count = layer_inputs.shape[0] * ndp
    rows, cols = left_inv.shape
    u, v, z, f = lax.axis_index("u"), lax.axis_index("v"), lax.axis_index("z"), lax.axis_index(F)

    padded = jnp.pad(weight_grad, ((0, PAD - rows), (0, 0)))
    weight_wide = lax.all_gather(padded, "z", axis=0, tiled=False)

    left_piece = swap_u_x(left_inv)

    act_local = jnp.sum(layer_inputs, axis=0, dtype=jnp.float32)
    grad_local = jnp.sum(out_grads, axis=0, dtype=jnp.float32)
    sums = share(jnp.concatenate([act_local, grad_local]), DP)
    means = jnp.sum(sums, axis=0) / token_count

    left_partial = jnp.sum(left_inv * means[None, :cols], axis=1)
    right_partial = jnp.sum(right_inv * means[cols:, None], axis=0)
    both = share(jnp.concatenate([means, left_partial, right_partial]), F)
    whole_act = both[:, :cols].reshape(nf * cols)
    whole_grad = both[:, cols : 2 * cols].reshape(nf * cols)
    images = jnp.sum(both[:, 2 * cols :], axis=0)
    left_piece, _ = lax.optimization_barrier((left_piece, images))
    left_wide = lax.all_gather(left_piece, F, axis=0, tiled=False)
    weight_wide, images = lax.optimization_barrier((weight_wide, images))
    weight_own = weight_wide[:, :rows, :].reshape(nz * rows, cols)
    weight_other = swap_v(weight_own)
    all_images = share(images, DP)
    left_image = all_images[:, :rows].reshape(ndp * rows)
    right_image = all_images[:, rows:].reshape(ndp * rows)
    left_coef = coefficient(jnp.sum(whole_act * left_image))
    right_coef = coefficient(jnp.sum(whole_grad * right_image))

    left_cols = block_of(left_image, f, cols)
    right_cols = block_of(right_image, f, cols)
    new_left = left_inv / decay - left_coef * images[:rows, None] * left_cols[None, :]
    new_right = right_inv / decay - right_coef * right_cols[:, None] * images[None, rows:]

    right_own = new_right.astype(jnp.bfloat16).T
    right_other = swap_v(right_own)
    right_pair = jnp.where(
        v == 0, jnp.stack([right_own, right_other]), jnp.stack([right_other, right_own])
    )
    right_half = lax.all_gather(right_pair, "z", axis=1, tiled=True)

    row_image = lax.dynamic_index_in_dim(
        left_image.reshape(nu, ndp // nu, rows), v * nz + z, 1, keepdims=False
    )
    left_wide = left_wide.reshape(nu, 2, rows, cols)

    def left_half(which):
        old = lax.dynamic_index_in_dim(left_wide, which, 1, keepdims=False)
        col_image = block_of(left_image, 2 * u + which, cols)
        new = old / decay - (left_coef * row_image[:, :, None]) * col_image[None, None, :]
        return new.astype(jnp.bfloat16).reshape(nu * rows, cols)

    partial = jnp.dot(left_half(v), weight_own, preferred_element_type=jnp.float32)
    partial += jnp.dot(left_half(1 - v), weight_other, preferred_element_type=jnp.float32)
    pieces = lax.all_to_all(partial.reshape(nu, rows, cols), "u", 0, 0, tiled=True)
    hidden_piece = jnp.sum(pieces, axis=0).astype(jnp.bfloat16)
    hidden = lax.all_gather(hidden_piece, "u", axis=0, tiled=True)

    partial = jnp.einsum(
        "crk,cmk->crm",
        jnp.broadcast_to(hidden[None], (2,) + hidden.shape),
        right_half,
        preferred_element_type=jnp.float32,
    )
    pieces = lax.all_to_all(partial, "c", 0, 0, tiled=True)
    partial = jnp.sum(pieces, axis=0)
    pieces = lax.all_to_all(partial.reshape(nu, rows, cols), "x", 0, 0, tiled=True)
    precond = jnp.sum(pieces, axis=0).astype(jnp.bfloat16)
    precond = swap_u_x(precond)
    return (precond, new_left, new_right)


def solution(mesh):
    cube = Mesh(mesh.devices.reshape(4, 2, 8, 4, 2), ("u", "v", "z", "x", "c"))
    rows, cols = P(DP, F), P(F, DP)

    return jax.shard_map(
        per_device,
        mesh=cube,
        in_specs=(rows, rows, rows, rows, cols),
        out_specs=(rows, rows, cols),
        check_vma=False,
    )
```

```python
import jax
import jax.numpy as jnp
from jax import lax
from jax.sharding import Mesh, PartitionSpec as P


decay = 0.9
PAD = 104
F = ("x", "c")
DP = ("u", "v", "z")


def coefficient(quadratic):
    return (1.0 - decay) / (decay * decay * (1.0 + (1.0 - decay) / decay * quadratic))


def share(vec, axes):
    count = lax.axis_size(axes)
    return lax.all_to_all(jnp.broadcast_to(vec[None], (count,) + vec.shape), axes, 0, 0, tiled=True)


def swap_u_x(block):
    n = lax.axis_size("u")
    return lax.ppermute(block, ("u", "x"), [(a * n + b, b * n + a) for a in range(n) for b in range(n)])


def swap_v(block):
    return lax.ppermute(block, "v", [(0, 1), (1, 0)])


def block_of(vec, index, size):
    return lax.dynamic_slice_in_dim(vec, index * size, size)


def per_device(layer_inputs, out_grads, weight_grad, left_inv, right_inv):
    nu, nz, nf, ndp = lax.axis_size("u"), lax.axis_size("z"), lax.axis_size(F), lax.axis_size(DP)
    token_count = layer_inputs.shape[0] * ndp
    rows, cols = left_inv.shape
    u, v, z, f = lax.axis_index("u"), lax.axis_index("v"), lax.axis_index("z"), lax.axis_index(F)

    padded = jnp.pad(weight_grad, ((0, PAD - rows), (0, 0)))
    weight_wide = lax.all_gather(padded, "z", axis=0, tiled=False)

    left_piece = swap_u_x(left_inv)

    right_own = right_inv.T
    right_other = swap_v(right_own)
    right_pair = jnp.where(
        v == 0, jnp.stack([right_own, right_other]), jnp.stack([right_other, right_own])
    )

    act_local = jnp.sum(layer_inputs, axis=0, dtype=jnp.float32)
    grad_local = jnp.sum(out_grads, axis=0, dtype=jnp.float32)
    sums = share(jnp.concatenate([act_local, grad_local]), DP)
    means = jnp.sum(sums, axis=0) / token_count

    left_partial = jnp.sum(left_inv * means[None, :cols], axis=1)
    right_partial = jnp.sum(right_inv * means[cols:, None], axis=0)
    both = share(jnp.concatenate([means, left_partial, right_partial]), F)
    whole_act = both[:, :cols].reshape(nf * cols)
    whole_grad = both[:, cols : 2 * cols].reshape(nf * cols)
    images = jnp.sum(both[:, 2 * cols :], axis=0)
    left_piece, _ = lax.optimization_barrier((left_piece, images))
    left_wide = lax.all_gather(left_piece, F, axis=0, tiled=False)
    weight_wide, images = lax.optimization_barrier((weight_wide, images))
    weight_own = weight_wide[:, :rows, :].reshape(nz * rows, cols)
    weight_other = swap_v(weight_own)
    all_images = share(images, DP)
    left_image = all_images[:, :rows].reshape(ndp * rows)
    right_image = all_images[:, rows:].reshape(ndp * rows)
    left_coef = coefficient(jnp.sum(whole_act * left_image))
    right_coef = coefficient(jnp.sum(whole_grad * right_image))

    left_cols = block_of(left_image, f, cols)
    right_cols = block_of(right_image, f, cols)
    new_left = left_inv / decay - left_coef * images[:rows, None] * left_cols[None, :]
    new_right = right_inv / decay - right_coef * right_cols[:, None] * images[None, rows:]

    pair_image = lax.dynamic_slice_in_dim(
        right_image.reshape(nu, 2, nz, rows), u, 1, 0
    )[0]
    pair_image = lax.dynamic_index_in_dim(pair_image, z, 1, keepdims=False)
    right_pair = right_pair / decay - (right_coef * right_cols) * pair_image[:, :, None]
    right_pair = right_pair.astype(jnp.bfloat16)
    right_half = lax.all_gather(right_pair, "z", axis=1, tiled=True)

    row_image = lax.dynamic_index_in_dim(
        left_image.reshape(nu, ndp // nu, rows), v * nz + z, 1, keepdims=False
    )
    left_wide = left_wide.reshape(nu, 2, rows, cols)

    def left_half(which):
        old = lax.dynamic_index_in_dim(left_wide, which, 1, keepdims=False)
        col_image = block_of(left_image, 2 * u + which, cols)
        new = old / decay - (left_coef * row_image[:, :, None]) * col_image[None, None, :]
        return new.astype(jnp.bfloat16).reshape(nu * rows, cols)

    partial = jnp.dot(left_half(v), weight_own, preferred_element_type=jnp.float32)
    partial += jnp.dot(left_half(1 - v), weight_other, preferred_element_type=jnp.float32)
    pieces = lax.all_to_all(partial.reshape(nu, rows, cols), "u", 0, 0, tiled=True)
    hidden_piece = jnp.sum(pieces, axis=0).astype(jnp.bfloat16)
    hidden = lax.all_gather(hidden_piece, "u", axis=0, tiled=True)

    partial = jnp.einsum(
        "crk,cmk->crm",
        jnp.broadcast_to(hidden[None], (2,) + hidden.shape),
        right_half,
        preferred_element_type=jnp.float32,
    )
    pieces = lax.all_to_all(partial, "c", 0, 0, tiled=True)
    partial = jnp.sum(pieces, axis=0)
    pieces = lax.all_to_all(partial.reshape(nu, rows, cols), "x", 0, 0, tiled=True)
    precond = jnp.sum(pieces, axis=0).astype(jnp.bfloat16)
    precond = swap_u_x(precond)
    return (precond, new_left, new_right)


def solution(mesh):
    cube = Mesh(mesh.devices.reshape(4, 2, 8, 4, 2), ("u", "v", "z", "x", "c"))
    rows, cols = P(DP, F), P(F, DP)

    return jax.shard_map(
        per_device,
        mesh=cube,
        in_specs=(rows, rows, rows, rows, cols),
        out_specs=(rows, rows, cols),
        check_vma=False,
    )
```
